128 devices in a mesh: row: 2 (over core), col: 2 (over x_lo), depth: 32 (over z, y, x_hi).
Axes of the slice: x: 4 (x_hi: 2, x_lo: 2; x = x_hi * 2 + x_lo), y: 4, z: 4, core: 2. Of those that a mesh axis runs over, the one named last changes fastest.
Arguments:
- left_blocks: bfloat16 [32, 2, 32, 2, 128, 128], P('col', 'row', 'depth'), may hold values from -0.625 to 0.625
- left_cols: int32 [32, 2, 32, 2], replicated, may hold values from 0 to 7, as said below
- right_blocks: bfloat16 [512, 2, 2, 128, 128], P(('col', 'depth'), 'row'), may hold values from -0.625 to 0.625
- right_cols: int32 [512, 2, 2], replicated, may hold values from 0 to 3, as said below
Outputs:
- product: float32 [4096, 1024], P(('col', 'depth'), 'row')
The draws below stay inside these ranges and needn't reach their ends.
Inputs may be any that keep to these rules, and one draw needn't show every extreme that they name: `left_cols`: within each group of 2 entries along the last dimension the values are distinct. `right_cols`: within each group of 2 entries along the last dimension the values are distinct.
All inputs are finite; a program needn't handle non-finite values.
Results may differ from the reference program's by a relative error of at most 0.0003.
Values may be sent and summed in bfloat16 or wider, within the bound.
A program may use at most 64 MiB of HBM per device.

```python
import jax
import jax.numpy as jnp
from jax import lax

BLK = 128
NBLK = 512
JB = 4
SA = 2
SB = 2
SECTIONS = 2
LAYERS = 32
COLGROUPS = 2
KPG = 8
ROWS_BLK = 32
COLS_BLK = 8


def pick_distinct(seed_key, lead_shape, pool_size, how_many):
    scores = jax.random.randint(seed_key, lead_shape + (pool_size,), 0, 1 << 20) * pool_size + jnp.arange(pool_size, dtype=jnp.int32)
    ranking = jnp.argsort(scores, axis=-1)
    return ranking[..., :how_many].astype(jnp.int32)


def draw_left_cols(key, part):
    return pick_distinct(jax.random.fold_in(key, 3), (ROWS_BLK, SECTIONS, LAYERS), KPG, SA)


def draw_right_cols(key, part):
    return pick_distinct(jax.random.fold_in(key, 7), (NBLK, COLGROUPS), JB, SB)


def block_scale(key, shape, cuts, low, high):
    gain = 1.0
    for dim, shards_of in cuts:
        draws = jax.random.uniform(jax.random.fold_in(jax.random.fold_in(key, 6), dim), (shards_of,), jnp.float32, low / len(cuts), high / len(cuts))
        gain = gain * jnp.repeat(jnp.exp(draws), shape[dim] // shards_of).reshape((-1,) + (1,) * (len(shape) - 1 - dim))
    return gain


def centred(own_key, shape, width, reach, shards=(), kind=jnp.bfloat16):
    level = block_scale(own_key, shape, shards, -0.22, 0.18) if shards else 1.0
    entries = jax.random.normal(own_key, shape, jnp.float32) * width * level
    return jnp.minimum(jnp.maximum(entries, -reach), reach).astype(kind)


def setup_inputs(seed: int = 0) -> dict:
    seeds = jax.random.split(jax.random.key(seed), 5)
    left_blocks = centred(seeds[0], (ROWS_BLK, SECTIONS, LAYERS, SA, BLK, BLK), ((BLK * SECTIONS * LAYERS * SA * SB // JB) ** -0.25), 0.625, ((0, 2), (1, 2), (2, 32)))
    left_cols = draw_left_cols(jax.random.fold_in(seeds[4], 71), 0)
    right_blocks = centred(seeds[2], (NBLK, COLGROUPS, SB, BLK, BLK), ((BLK * SECTIONS * LAYERS * SA * SB // JB) ** -0.25), 0.625, ((0, 64), (1, 2)))
    right_cols = draw_right_cols(jax.random.fold_in(seeds[4], 71), 0)
    return dict(left_blocks=left_blocks, left_cols=left_cols, right_blocks=right_blocks, right_cols=right_cols)


def reference(left_blocks, left_cols, right_blocks, right_cols):
    groups = jnp.arange(SECTIONS, dtype=jnp.int32)
    offsets = (groups[:, None] * LAYERS + jnp.arange(LAYERS, dtype=jnp.int32)[None, :]) * KPG
    levels = jnp.arange(JB, dtype=jnp.int32)

    def one_row(inputs):
        blocks, columns = inputs
        block_cols = (offsets[:, :, None] + columns.astype(jnp.int32)).reshape(-1)
        rows_right = jnp.take(right_blocks, block_cols, axis=0).astype(jnp.float32)
        right_index = jnp.take(right_cols, block_cols, axis=0).astype(jnp.int32)
        chooser = (right_index[..., None] == levels).astype(jnp.float32)
        spread = jnp.einsum('mgbl,mgbyz->mglyz', chooser, rows_right, precision=lax.Precision.HIGHEST)
        left_flat = blocks.reshape(-1, BLK, BLK).astype(jnp.float32)
        result = jnp.einsum('mxy,mglyz->xglz', left_flat, spread, precision=lax.Precision.HIGHEST)
        return result.reshape(BLK, COLGROUPS * JB * BLK)

    row_blocks = lax.map(one_row, (left_blocks, left_cols))
    return row_blocks.reshape(ROWS_BLK * BLK, COLS_BLK * BLK).astype(jnp.float32)
```

```python
import jax
import jax.numpy as jnp
from jax import lax
from jax.experimental import pallas as pl
from jax.experimental.pallas import tpu as pltpu
from jax.sharding import PartitionSpec as P

BLK = 128
JB = 4
PASSES = 2
WIDTH = BLK // PASSES
NCOL = JB * WIDTH
ROWS = 16
KPG = 8
HALF = BLK // 2
TOP = 32767.0
MESH = pl.DeviceIdType.MESH


def coded(x, axes):
    peak = jnp.maximum(jnp.max(jnp.abs(x), axis=axes, keepdims=True), 1e-33)
    whole = jnp.round(x * (TOP / peak)).astype(jnp.int32).astype(jnp.int16)
    return whole, peak.reshape(1, NCOL) * (1.0 / TOP)


def decoded(whole, scale):
    return whole.astype(jnp.int32).astype(jnp.float32) * scale


def kernel(idx, left_hbm, right, out, left, packed, other, spread, acc, ubuf,
           q1s, q1r, s1s, s1r, q2s, q2r, s2s, s2r, q3s, q3r, s3s, s3r,
           lsem, xs, xr, a1s, a1r, b1s, b1r, a2s, a2r, b2s, b2r, a3s, a3r, b3s, b3r):
    r = lax.axis_index("row")
    c = lax.axis_index("col")
    d = lax.axis_index("depth")
    z, y, h = d // 8, (d // 2) % 4, d % 2

    def at(zz, yy, hh):
        return (r, c, (zz % 4) * 8 + (yy % 4) * 2 + hh)

    mate, peer, far = (1 - r, c, d), (r, 1 - c, d), at(z, y, 1 - h)
    along = (
        lambda by: at(z + by, y, h),
        lambda by: at(z, y + by, h),
    )
    barrier = pltpu.get_barrier_semaphore()
    peers = [mate, peer, far] + [go(by) for go in along for by in (1, 2, 3)]
    for device in peers:
        pl.semaphore_signal(barrier, inc=1, device_id=device, device_id_type=MESH)

    started = []

    def send(src, dst, ssem, rsem, device):
        copy = pltpu.make_async_remote_copy(
            src_ref=src, dst_ref=dst, send_sem=ssem, recv_sem=rsem,
            device_id=device, device_id_type=MESH)
        copy.start()
        started.append(copy)

    def arrived(src, dst, ssem, rsem):
        pltpu.make_async_remote_copy(
            src_ref=src, dst_ref=dst, send_sem=ssem, recv_sem=rsem,
            device_id=mate, device_id_type=MESH).wait_recv()

    mine = pltpu.make_async_copy(left_hbm, left.at[0], lsem)
    mine.start()

    low = lax.broadcasted_iota(jnp.int32, (BLK, BLK), 1) < HALF

    for k in range(KPG):
        one, two = right[k, 0], right[k, 1]
        packed[0, k] = jnp.concatenate([one[:, :HALF], two[:, :HALF]], axis=1)
        packed[1, k] = jnp.concatenate([one[:, HALF:], two[:, HALF:]], axis=1)

    pl.semaphore_wait(barrier, len(peers))
    for s in range(PASSES):
        send(packed.at[s], other.at[s], xs.at[s], xr.at[s], peer)
    send(left_hbm, left.at[1], xs.at[2], xr.at[2], mate)

    lane = lax.broadcasted_iota(jnp.int32, (1, BLK), 1)
    upper = (lane >= HALF).astype(jnp.int32)

    def widen(block, group, k):
        base = ROWS * 4 + (group * KPG + k) * 2
        j0, j1 = idx[base], idx[base + 1]
        turned = pltpu.roll(block, HALF, 1)
        straight = jnp.where(upper == 0, j0, j1)
        crossed = jnp.where(upper == 0, j1, j0)
        for t in range(2):
            target = upper + 2 * t
            keep = (straight == target).astype(jnp.float32).astype(jnp.bfloat16)
            swap = (crossed == target).astype(jnp.float32).astype(jnp.bfloat16)
            spread[group * KPG + k, :, t * BLK:(t + 1) * BLK] = block * keep + turned * swap

    def multiply(s):
        @pl.loop(0, ROWS // 4)
        def _(block_z):
            for block_y in range(4):
                i = block_z * 4 + block_y
                total = None
                for slot, group in ((0, r), (1, 1 - r)):
                    base = (i * 2 + group) * 2
                    a0, a1 = idx[base], idx[base + 1]
                    lhs = jnp.concatenate([left[slot, i, 0], left[slot, i, 1]], axis=1)
                    rhs = jnp.concatenate([spread[group * KPG + a0], spread[group * KPG + a1]], axis=0)
                    term = jnp.dot(lhs, rhs, preferred_element_type=jnp.float32)
                    total = term if total is None else total + term
                acc[s, block_z, block_y] = total

    where = (z, y)

    def own(s, part, pair, dest):
        if part == 0:
            return acc[s, dest, 2 * pair:2 * pair + 2, :HALF, :]
        return acc[s, 2 * pair:2 * pair + 2, dest, HALF:, :]

    def one(s, part, w, dest):
        if part == 0:
            return acc[s, dest, w, :HALF, :]
        return acc[s, w, dest, HALF:, :]

    def post1(s, part, slot, value, by):
        whole, scale = coded(value, (0, 1))
        q1s[s, part, slot] = whole
        s1s[s, part, slot] = scale
        n = (s * 2 + part) * 6 + slot
        send(q1s.at[s, part, slot], q1r.at[s, part, slot], a1s.at[n], a1r.at[n], along[part](by))
        send(s1s.at[s, part, slot], s1r.at[s, part, slot], b1s.at[n], b1r.at[n], along[part](by))

    def got1(s, part, slot):
        n = (s * 2 + part) * 6 + slot
        arrived(q1s.at[s, part, slot], q1r.at[s, part, slot], a1s.at[n], a1r.at[n])
        arrived(s1s.at[s, part, slot], s1r.at[s, part, slot], b1s.at[n], b1r.at[n])

    def stage1_open(s):
        for part in range(2):
            v = where[part]
            post1(s, part, 0, own(s, part, 0, (v + 2) % 4), 1)
            post1(s, part, 1, own(s, part, 1, (v + 2) % 4), 3)
        for part in range(2):
            v = where[part]
            post1(s, part, 3, own(s, part, 1, (v + 1) % 4), 1)
            post1(s, part, 4, own(s, part, 0, (v + 3) % 4), 3)

    def stage1_relay(s):
        for part in range(2):
            v = where[part]
            for slot, pair, by in ((0, 0, 1), (1, 1, 3)):
                got1(s, part, slot)
                value = own(s, part, pair, (v + by) % 4) + decoded(q1r[s, part, slot], s1r[s, part, slot])
                post1(s, part, 2 if slot == 0 else 5, value, by)

    def reduced(s, part, w):
        value = one(s, part, w, where[part])
        for first in (2, 4):
            pair = first + w // 2
            value = value + decoded(q1r[s, part, pair, w % 2], s1r[s, part, pair])
        return value

    def stage2(s):
        for part in range(2):
            for slot in (3, 4, 2, 5):
                got1(s, part, slot)
            v = where[1 - part]
            for by in (2, 1, 3):
                whole, scale = coded(reduced(s, part, (v + by) % 4), 0)
                q2s[s, part, by - 1] = whole
                s2s[s, part, by - 1] = scale
                n = (s * 2 + part) * 3 + by - 1
                send(q2s.at[s, part, by - 1], q2r.at[s, part, by - 1], a2s.at[n], a2r.at[n], along[1 - part](by))
                send(s2s.at[s, part, by - 1], s2r.at[s, part, by - 1], b2s.at[n], b2r.at[n], along[1 - part](by))
            ubuf[s, part] = reduced(s, part, v)

    def stage3(s):
        for part in range(2):
            value = ubuf[s, part]
            for by in range(3):
                n = (s * 2 + part) * 3 + by
                arrived(q2s.at[s, part, by], q2r.at[s, part, by], a2s.at[n], a2r.at[n])
                arrived(s2s.at[s, part, by], s2r.at[s, part, by], b2s.at[n], b2r.at[n])
                value = value + decoded(q2r[s, part, by], s2r[s, part, by])
            ubuf[s, part] = value
        whole, scale = coded(ubuf[s, 1 - h], 0)
        q3s[s] = whole
        s3s[s] = scale
        send(q3s.at[s], q3r.at[s], a3s.at[s], a3r.at[s], far)
        send(s3s.at[s], s3r.at[s], b3s.at[s], b3r.at[s], far)

    def final(s):
        arrived(q3s.at[s], q3r.at[s], a3s.at[s], a3r.at[s])
        arrived(s3s.at[s], s3r.at[s], b3s.at[s], b3r.at[s])
        return ubuf[s, h] + decoded(q3r[s], s3r[s])

    def prepare(s):
        @pl.loop(0, KPG)
        def _(k):
            widen(packed[s, k], c, k)

    def finish(s):
        arrived(packed.at[s], other.at[s], xs.at[s], xr.at[s])

        @pl.loop(0, KPG)
        def _(k):
            widen(other[s, k], 1 - c, k)
        multiply(s)

    prepare(0)
    mine.wait()
    arrived(left_hbm, left.at[1], xs.at[2], xr.at[2])
    finish(0)
    stage1_open(0)
    prepare(1)
    stage1_relay(0)
    finish(1)
    stage1_open(1)
    stage2(0)
    stage1_relay(1)
    stage3(0)
    stage2(1)
    first = final(0)
    stage3(1)
    second = final(1)
    for j in range(JB):
        out[:, j * BLK:(j + 1) * BLK] = jnp.concatenate(
            [first[:, j * WIDTH:(j + 1) * WIDTH], second[:, j * WIDTH:(j + 1) * WIDTH]], axis=1)
    for copy in started:
        copy.wait_send()


def local(left_blocks, left_cols, right_blocks, right_cols):
    r = lax.axis_index("row")
    c = lax.axis_index("col")
    d = lax.axis_index("depth")
    rows_idx = lax.dynamic_slice(left_cols, (c * ROWS, 0, d, 0), (ROWS, 2, 1, 2)).reshape(-1)
    by_layer = right_cols.reshape(2, 32, KPG, 2, 2)
    right_idx = lax.dynamic_slice(by_layer, (0, d, 0, r, 0), (2, 1, KPG, 1, 2)).reshape(-1)
    idx = jnp.concatenate([rows_idx, right_idx])
    dma = pltpu.SemaphoreType.DMA
    vmem = pltpu.VMEM
    q1 = vmem((PASSES, 2, 6, 2, HALF, NCOL), jnp.int16)
    s1 = vmem((PASSES, 2, 6, 1, NCOL), jnp.float32)
    q2 = vmem((PASSES, 2, 3, HALF, NCOL), jnp.int16)
    s2 = vmem((PASSES, 2, 3, 1, NCOL), jnp.float32)
    q3 = vmem((PASSES, HALF, NCOL), jnp.int16)
    s3 = vmem((PASSES, 1, NCOL), jnp.float32)
    n1, n2, n3 = PASSES * 12, PASSES * 6, PASSES
    return pl.pallas_call(
        kernel,
        out_shape=jax.ShapeDtypeStruct((HALF, JB * BLK), jnp.float32),
        in_specs=[
            pl.BlockSpec(memory_space=pltpu.SMEM),
            pl.BlockSpec(memory_space=pl.ANY),
            pl.BlockSpec(memory_space=pltpu.VMEM),
        ],
        out_specs=pl.BlockSpec(memory_space=pltpu.VMEM),
        scratch_shapes=[
            vmem((2, ROWS, 2, BLK, BLK), jnp.bfloat16),
            vmem((PASSES, KPG, BLK, BLK), jnp.bfloat16),
            vmem((PASSES, KPG, BLK, BLK), jnp.bfloat16),
            vmem((2 * KPG, BLK, NCOL), jnp.bfloat16),
            vmem((PASSES, 4, 4, BLK, NCOL), jnp.float32),
            vmem((PASSES, 2, HALF, NCOL), jnp.float32),
            q1, q1, s1, s1, q2, q2, s2, s2, q3, q3, s3, s3,
            dma, dma((3,)), dma((3,)),
            dma((n1,)), dma((n1,)), dma((n1,)), dma((n1,)),
            dma((n2,)), dma((n2,)), dma((n2,)), dma((n2,)),
            dma((n3,)), dma((n3,)), dma((n3,)), dma((n3,)),
        ],
        compiler_params=pltpu.CompilerParams(
            collective_id=0, has_side_effects=True, vmem_limit_bytes=48 << 20),
    )(idx, left_blocks.reshape(ROWS, 2, BLK, BLK), right_blocks.reshape(KPG, 2, BLK, BLK))


def solution(mesh):
    return jax.shard_map(
        local,
        mesh=mesh,
        in_specs=(
            P("col", "row", "depth", None, None, None),
            P(),
            P(("col", "depth"), "row", None, None, None),
            P(),
        ),
        out_specs=P(("col", "depth"), "row"),
        check_vma=False,
    )
```

```python
import jax
import jax.numpy as jnp
from jax import lax
from jax.experimental import pallas as pl
from jax.experimental.pallas import tpu as pltpu
from jax.sharding import PartitionSpec as P

BLK = 128
JB = 4
PASSES = 2
WIDTH = BLK // PASSES
NCOL = JB * WIDTH
ROWS = 16
KPG = 8
HALF = BLK // 2
TOP = 32767.0
MESH = pl.DeviceIdType.MESH


def coded(x, axes):
    peak = jnp.maximum(jnp.max(jnp.abs(x), axis=axes, keepdims=True), 1e-33)
    whole = jnp.round(x * (TOP / peak)).astype(jnp.int32).astype(jnp.int16)
    return whole, peak.reshape(1, NCOL) * (1.0 / TOP)


def decoded(whole, scale):
    return whole.astype(jnp.int32).astype(jnp.float32) * scale


def kernel(lcols_hbm, rcols_hbm, left_hbm, right_hbm, out, lcols, rcols, right, left, packed, other, spread, acc, ubuf,
           q1s, q1r, s1s, s1r, q2s, q2r, s2s, s2r, q3s, q3r, s3s, s3r,
           lsem, isem, xs, xr, a1s, a1r, b1s, b1r, a2s, a2r, b2s, b2r, a3s, a3r, b3s, b3r):
    r = lax.axis_index("row")
    c = lax.axis_index("col")
    d = lax.axis_index("depth")
    z, y, h = d // 8, (d // 2) % 4, d % 2

    def at(zz, yy, hh):
        return (r, c, (zz % 4) * 8 + (yy % 4) * 2 + hh)

    mate, peer, far = (1 - r, c, d), (r, 1 - c, d), at(z, y, 1 - h)
    along = (
        lambda by: at(z + by, y, h),
        lambda by: at(z, y + by, h),
    )
    mine = pltpu.make_async_copy(left_hbm, left.at[0], lsem.at[0])
    margin = pltpu.make_async_copy(right_hbm, right, lsem.at[1])
    left_index = pltpu.make_async_copy(lcols_hbm.at[pl.ds(c * ROWS, ROWS)], lcols, isem.at[0])
    right_index = pltpu.make_async_copy(rcols_hbm, rcols, isem.at[1])
    margin.start()
    mine.start()
    left_index.start()
    right_index.start()

    barrier = pltpu.get_barrier_semaphore()
    peers = [mate, peer, far] + [go(by) for go in along for by in (1, 2, 3)]
    for device in peers:
        pl.semaphore_signal(barrier, inc=1, device_id=device, device_id_type=MESH)

    started = []

    def send(src, dst, ssem, rsem, device):
        copy = pltpu.make_async_remote_copy(
            src_ref=src, dst_ref=dst, send_sem=ssem, recv_sem=rsem,
            device_id=device, device_id_type=MESH)
        copy.start()
        started.append(copy)

    def arrived(src, dst, ssem, rsem):
        pltpu.make_async_remote_copy(
            src_ref=src, dst_ref=dst, send_sem=ssem, recv_sem=rsem,
            device_id=mate, device_id_type=MESH).wait_recv()

    margin.wait()
    for k in range(KPG):
        one, two = right[k, 0], right[k, 1]
        packed[0, k] = jnp.concatenate([one[:, :HALF], two[:, :HALF]], axis=1)
        packed[1, k] = jnp.concatenate([one[:, HALF:], two[:, HALF:]], axis=1)

    pl.semaphore_wait(barrier, len(peers))
    for s in range(PASSES):
        send(packed.at[s], other.at[s], xs.at[s], xr.at[s], peer)
    send(left_hbm, left.at[1], xs.at[2], xr.at[2], mate)

    lane = lax.broadcasted_iota(jnp.int32, (1, BLK), 1)
    upper = (lane >= HALF).astype(jnp.int32)

    def widen(block, group, k):
        row = group * (32 * KPG) + d * KPG + k
        j0, j1 = rcols[r, 0, row], rcols[r, 1, row]
        turned = pltpu.roll(block, HALF, 1)
        straight = jnp.where(upper == 0, j0, j1)
        crossed = jnp.where(upper == 0, j1, j0)
        for t in range(2):
            target = upper + 2 * t
            keep = (straight == target).astype(jnp.float32).astype(jnp.bfloat16)
            swap = (crossed == target).astype(jnp.float32).astype(jnp.bfloat16)
            spread[group * KPG + k, :, t * BLK:(t + 1) * BLK] = block * keep + turned * swap

    def multiply(s, group, add):
        slot = (group + r) % 2

        @pl.loop(0, ROWS // 4)
        def _(block_z):
            for block_y in range(4):
                i = block_z * 4 + block_y
                a0, a1 = lcols[i, group, 0, d], lcols[i, group, 1, d]
                lhs = jnp.concatenate([left[slot, i, 0], left[slot, i, 1]], axis=1)
                rhs = jnp.concatenate([spread[group * KPG + a0], spread[group * KPG + a1]], axis=0)
                term = jnp.dot(lhs, rhs, preferred_element_type=jnp.float32)
                if add:
                    term = term + acc[s, block_z, block_y]
                acc[s, block_z, block_y] = term

    where = (z, y)

    def own(s, part, pair, dest):
        if part == 0:
            return acc[s, dest, 2 * pair:2 * pair + 2, :HALF, :]
        return acc[s, 2 * pair:2 * pair + 2, dest, HALF:, :]

    def one(s, part, w, dest):
        if part == 0:
            return acc[s, dest, w, :HALF, :]
        return acc[s, w, dest, HALF:, :]

    def post1(s, part, slot, value, by):
        whole, scale = coded(value, (0, 1))
        q1s[s, part, slot] = whole
        s1s[s, part, slot] = scale
        n = (s * 2 + part) * 6 + slot
        send(q1s.at[s, part, slot], q1r.at[s, part, slot], a1s.at[n], a1r.at[n], along[part](by))
        send(s1s.at[s, part, slot], s1r.at[s, part, slot], b1s.at[n], b1r.at[n], along[part](by))

    def got1(s, part, slot):
        n = (s * 2 + part) * 6 + slot
        arrived(q1s.at[s, part, slot], q1r.at[s, part, slot], a1s.at[n], a1r.at[n])
        arrived(s1s.at[s, part, slot], s1r.at[s, part, slot], b1s.at[n], b1r.at[n])

    def stage1_open(s):
        for part in range(2):
            v = where[part]
            post1(s, part, 0, own(s, part, 0, (v + 2) % 4), 1)
            post1(s, part, 1, own(s, part, 1, (v + 2) % 4), 3)
        for part in range(2):
            v = where[part]
            post1(s, part, 3, own(s, part, 1, (v + 1) % 4), 1)
            post1(s, part, 4, own(s, part, 0, (v + 3) % 4), 3)

    def stage1_relay(s):
        for part in range(2):
            v = where[part]
            for slot, pair, by in ((0, 0, 1), (1, 1, 3)):
                got1(s, part, slot)
                value = own(s, part, pair, (v + by) % 4) + decoded(q1r[s, part, slot], s1r[s, part, slot])
                post1(s, part, 2 if slot == 0 else 5, value, by)

    def reduced(s, part, w):
        value = one(s, part, w, where[part])
        for first in (2, 4):
            pair = first + w // 2
            value = value + decoded(q1r[s, part, pair, w % 2], s1r[s, part, pair])
        return value

    def stage2(s):
        for part in range(2):
            for slot in (3, 4, 2, 5):
                got1(s, part, slot)
            v = where[1 - part]
            for by in (2, 1, 3):
                whole, scale = coded(reduced(s, part, (v + by) % 4), 0)
                q2s[s, part, by - 1] = whole
                s2s[s, part, by - 1] = scale
                n = (s * 2 + part) * 3 + by - 1
                send(q2s.at[s, part, by - 1], q2r.at[s, part, by - 1], a2s.at[n], a2r.at[n], along[1 - part](by))
                send(s2s.at[s, part, by - 1], s2r.at[s, part, by - 1], b2s.at[n], b2r.at[n], along[1 - part](by))
            ubuf[s, part] = reduced(s, part, v)

    def stage3(s):
        for part in range(2):
            value = ubuf[s, part]
            for by in range(3):
                n = (s * 2 + part) * 3 + by
                arrived(q2s.at[s, part, by], q2r.at[s, part, by], a2s.at[n], a2r.at[n])
                arrived(s2s.at[s, part, by], s2r.at[s, part, by], b2s.at[n], b2r.at[n])
                value = value + decoded(q2r[s, part, by], s2r[s, part, by])
            ubuf[s, part] = value
        whole, scale = coded(ubuf[s, 1 - h], 0)
        q3s[s] = whole
        s3s[s] = scale
        send(q3s.at[s], q3r.at[s], a3s.at[s], a3r.at[s], far)
        send(s3s.at[s], s3r.at[s], b3s.at[s], b3r.at[s], far)

    def final(s):
        arrived(q3s.at[s], q3r.at[s], a3s.at[s], a3r.at[s])
        arrived(s3s.at[s], s3r.at[s], b3s.at[s], b3r.at[s])
        return ubuf[s, h] + decoded(q3r[s], s3r[s])

    def begin(s):
        @pl.loop(0, KPG)
        def _(k):
            widen(packed[s, k], c, k)
        multiply(s, c, False)

    def finish(s):
        arrived(packed.at[s], other.at[s], xs.at[s], xr.at[s])

        @pl.loop(0, KPG)
        def _(k):
            widen(other[s, k], 1 - c, k)
        multiply(s, 1 - c, True)

    left_index.wait()
    right_index.wait()
    mine.wait()
    arrived(left_hbm, left.at[1], xs.at[2], xr.at[2])
    begin(0)
    begin(1)
    finish(0)
    stage1_open(0)
    stage1_relay(0)
    finish(1)
    stage1_open(1)
    stage2(0)
    stage1_relay(1)
    stage3(0)
    stage2(1)
    first = final(0)
    stage3(1)
    second = final(1)
    for j in range(JB):
        out[:, j * BLK:(j + 1) * BLK] = jnp.concatenate(
            [first[:, j * WIDTH:(j + 1) * WIDTH], second[:, j * WIDTH:(j + 1) * WIDTH]], axis=1)
    for copy in started:
        copy.wait_send()


def local(left_blocks, left_cols, right_blocks, right_cols):
    dma = pltpu.SemaphoreType.DMA
    vmem = pltpu.VMEM
    q1 = vmem((PASSES, 2, 6, 2, HALF, NCOL), jnp.int16)
    s1 = vmem((PASSES, 2, 6, 1, NCOL), jnp.float32)
    q2 = vmem((PASSES, 2, 3, HALF, NCOL), jnp.int16)
    s2 = vmem((PASSES, 2, 3, 1, NCOL), jnp.float32)
    q3 = vmem((PASSES, HALF, NCOL), jnp.int16)
    s3 = vmem((PASSES, 1, NCOL), jnp.float32)
    n1, n2, n3 = PASSES * 12, PASSES * 6, PASSES
    return pl.pallas_call(
        kernel,
        out_shape=jax.ShapeDtypeStruct((HALF, JB * BLK), jnp.float32),
        in_specs=[pl.BlockSpec(memory_space=pl.ANY)] * 4,
        out_specs=pl.BlockSpec(memory_space=pltpu.VMEM),
        scratch_shapes=[
            pltpu.SMEM((ROWS, 2, 2, 32), jnp.int32),
            pltpu.SMEM((2, 2, 2 * 32 * KPG), jnp.int32),
            vmem((KPG, 2, BLK, BLK), jnp.bfloat16),
            vmem((2, ROWS, 2, BLK, BLK), jnp.bfloat16),
            vmem((PASSES, KPG, BLK, BLK), jnp.bfloat16),
            vmem((PASSES, KPG, BLK, BLK), jnp.bfloat16),
            vmem((2 * KPG, BLK, NCOL), jnp.bfloat16),
            vmem((PASSES, 4, 4, BLK, NCOL), jnp.float32),
            vmem((PASSES, 2, HALF, NCOL), jnp.float32),
            q1, q1, s1, s1, q2, q2, s2, s2, q3, q3, s3, s3,
            dma((2,)), dma((2,)), dma((3,)), dma((3,)),
            dma((n1,)), dma((n1,)), dma((n1,)), dma((n1,)),
            dma((n2,)), dma((n2,)), dma((n2,)), dma((n2,)),
            dma((n3,)), dma((n3,)), dma((n3,)), dma((n3,)),
        ],
        compiler_params=pltpu.CompilerParams(
            collective_id=0, has_side_effects=True, vmem_limit_bytes=67_043_328),
    )(left_cols.transpose(0, 1, 3, 2), right_cols.transpose(1, 2, 0), left_blocks.reshape(ROWS, 2, BLK, BLK), right_blocks.reshape(KPG, 2, BLK, BLK))


def solution(mesh):
    return jax.shard_map(
        local,
        mesh=mesh,
        in_specs=(
            P("col", "row", "depth", None, None, None),
            P(),
            P(("col", "depth"), "row", None, None, None),
            P(),
        ),
        out_specs=P(("col", "depth"), "row"),
        check_vma=False,
    )
```

```python
import jax
import jax.numpy as jnp
from jax import lax
from jax.experimental import pallas as pl
from jax.experimental.pallas import tpu as pltpu
from jax.sharding import PartitionSpec as P

BLK = 128
JB = 4
PASSES = 4
WIDTH = BLK // PASSES
NCOL = JB * WIDTH
ROWS = 16
KPG = 8
HALF = BLK // 2
TOP = 32767.0
MESH = pl.DeviceIdType.MESH


def coded(x, axes):
    peak = jnp.maximum(jnp.max(jnp.abs(x), axis=axes, keepdims=True), 1e-33)
    whole = jnp.round(x * (TOP / peak)).astype(jnp.int32).astype(jnp.int16)
    return whole, peak.reshape(1, NCOL) * (1.0 / TOP)


def decoded(whole, scale):
    return whole.astype(jnp.int32).astype(jnp.float32) * scale


def kernel(lcols_hbm, rcols_hbm, left_hbm, right_hbm, out, lcols, rcols, right, left, packed, other, spread, acc, ubuf,
           q1s, q1r, s1s, s1r, q2s, q2r, s2s, s2r, q3s, q3r, s3s, s3r,
           lsem, isem, xs, xr, a1s, a1r, b1s, b1r, a2s, a2r, b2s, b2r, a3s, a3r, b3s, b3r):
    r = lax.axis_index("row")
    c = lax.axis_index("col")
    d = lax.axis_index("depth")
    z, y, h = d // 8, (d // 2) % 4, d % 2

    def at(zz, yy, hh):
        return (r, c, (zz % 4) * 8 + (yy % 4) * 2 + hh)

    mate, peer, far = (1 - r, c, d), (r, 1 - c, d), at(z, y, 1 - h)
    along = (
        lambda by: at(z + by, y, h),
        lambda by: at(z, y + by, h),
    )
    mine = pltpu.make_async_copy(left_hbm, left.at[0], lsem.at[0])
    margin = pltpu.make_async_copy(right_hbm, right, lsem.at[1])
    left_index = pltpu.make_async_copy(lcols_hbm.at[pl.ds(c * ROWS, ROWS)], lcols, isem.at[0])
    right_index = pltpu.make_async_copy(rcols_hbm, rcols, isem.at[1])
    margin.start()
    mine.start()
    left_index.start()
    right_index.start()

    barrier = pltpu.get_barrier_semaphore()
    peers = [mate, peer, far] + [go(by) for go in along for by in (1, 2, 3)]
    for device in peers:
        pl.semaphore_signal(barrier, inc=1, device_id=device, device_id_type=MESH)

    started = []

    def send(src, dst, ssem, rsem, device):
        copy = pltpu.make_async_remote_copy(
            src_ref=src, dst_ref=dst, send_sem=ssem, recv_sem=rsem,
            device_id=device, device_id_type=MESH)
        copy.start()
        started.append(copy)

    def arrived(src, dst, ssem, rsem):
        pltpu.make_async_remote_copy(
            src_ref=src, dst_ref=dst, send_sem=ssem, recv_sem=rsem,
            device_id=mate, device_id_type=MESH).wait_recv()

    margin.wait()
    for k in range(0, KPG, 2):
        blocks = [right[k, 0], right[k, 1], right[k + 1, 0], right[k + 1, 1]]
        for s in range(PASSES):
            packed[s, k // 2] = jnp.concatenate([b[:, s * WIDTH:(s + 1) * WIDTH] for b in blocks], axis=1)

    pl.semaphore_wait(barrier, len(peers))
    for s in range(PASSES):
        send(packed.at[s], other.at[s], xs.at[s], xr.at[s], peer)
    send(left_hbm, left.at[1], xs.at[PASSES], xr.at[PASSES], mate)

    target = lax.broadcasted_iota(jnp.int32, (1, BLK), 1) // WIDTH

    def widen(two_rows, group, pair):
        turned = [two_rows] + [pltpu.roll(two_rows, by * WIDTH, 1) for by in range(1, JB)]
        for odd in range(2):
            k = 2 * pair + odd
            row = group * (32 * KPG) + d * KPG + k
            j0, j1 = rcols[r, 0, row], rcols[r, 1, row]
            turn = jnp.where(target == j0, (target - 2 * odd) & 3,
                             jnp.where(target == j1, (target - 2 * odd - 1) & 3, -1))
            total = None
            for by in range(JB):
                term = turned[by] * (turn == by).astype(jnp.float32).astype(jnp.bfloat16)
                total = term if total is None else total + term
            spread[group * KPG + k] = total

    def multiply(s, group, add):
        slot = (group + r) % 2

        @pl.loop(0, ROWS // 4)
        def _(block_z):
            for block_y in range(4):
                i = block_z * 4 + block_y
                a0, a1 = lcols[i, group, 0, d], lcols[i, group, 1, d]
                lhs = jnp.concatenate([left[slot, i, 0], left[slot, i, 1]], axis=1)
                rhs = jnp.concatenate([spread[group * KPG + a0], spread[group * KPG + a1]], axis=0)
                term = jnp.dot(lhs, rhs, preferred_element_type=jnp.float32)
                if add:
                    term = term + acc[s, block_z, block_y]
                acc[s, block_z, block_y] = term

    where = (z, y)

    def own(s, part, pair, dest):
        if part == 0:
            return acc[s, dest, 2 * pair:2 * pair + 2, :HALF, :]
        return acc[s, 2 * pair:2 * pair + 2, dest, HALF:, :]

    def one(s, part, w, dest):
        if part == 0:
            return acc[s, dest, w, :HALF, :]
        return acc[s, w, dest, HALF:, :]

    def post1(s, part, slot, value, by):
        whole, scale = coded(value, (0, 1))
        q1s[s, part, slot] = whole
        s1s[s, part, slot] = scale
        n = (s * 2 + part) * 6 + slot
        send(q1s.at[s, part, slot], q1r.at[s, part, slot], a1s.at[n], a1r.at[n], along[part](by))
        send(s1s.at[s, part, slot], s1r.at[s, part, slot], b1s.at[n], b1r.at[n], along[part](by))

    def got1(s, part, slot):
        n = (s * 2 + part) * 6 + slot
        arrived(q1s.at[s, part, slot], q1r.at[s, part, slot], a1s.at[n], a1r.at[n])
        arrived(s1s.at[s, part, slot], s1r.at[s, part, slot], b1s.at[n], b1r.at[n])

    def stage1_open(s):
        for part in range(2):
            v = where[part]
            post1(s, part, 0, own(s, part, 0, (v + 2) % 4), 1)
            post1(s, part, 1, own(s, part, 1, (v + 2) % 4), 3)
        for part in range(2):
            v = where[part]
            post1(s, part, 3, own(s, part, 1, (v + 1) % 4), 1)
            post1(s, part, 4, own(s, part, 0, (v + 3) % 4), 3)

    def stage1_relay(s):
        for part in range(2):
            v = where[part]
            for slot, pair, by in ((0, 0, 1), (1, 1, 3)):
                got1(s, part, slot)
                value = own(s, part, pair, (v + by) % 4) + decoded(q1r[s, part, slot], s1r[s, part, slot])
                post1(s, part, 2 if slot == 0 else 5, value, by)

    def reduced(s, part, w):
        value = one(s, part, w, where[part])
        for first in (2, 4):
            pair = first + w // 2
            value = value + decoded(q1r[s, part, pair, w % 2], s1r[s, part, pair])
        return value

    def stage2(s):
        for part in range(2):
            for slot in (3, 4, 2, 5):
                got1(s, part, slot)
            v = where[1 - part]
            for by in (2, 1, 3):
                whole, scale = coded(reduced(s, part, (v + by) % 4), 0)
                q2s[s, part, by - 1] = whole
                s2s[s, part, by - 1] = scale
                n = (s * 2 + part) * 3 + by - 1
                send(q2s.at[s, part, by - 1], q2r.at[s, part, by - 1], a2s.at[n], a2r.at[n], along[1 - part](by))
                send(s2s.at[s, part, by - 1], s2r.at[s, part, by - 1], b2s.at[n], b2r.at[n], along[1 - part](by))
            ubuf[s, part] = reduced(s, part, v)

    def stage3(s):
        for part in range(2):
            value = ubuf[s, part]
            for by in range(3):
                n = (s * 2 + part) * 3 + by
                arrived(q2s.at[s, part, by], q2r.at[s, part, by], a2s.at[n], a2r.at[n])
                arrived(s2s.at[s, part, by], s2r.at[s, part, by], b2s.at[n], b2r.at[n])
                value = value + decoded(q2r[s, part, by], s2r[s, part, by])
            ubuf[s, part] = value
        whole, scale = coded(ubuf[s, 1 - h], 0)
        q3s[s] = whole
        s3s[s] = scale
        send(q3s.at[s], q3r.at[s], a3s.at[s], a3r.at[s], far)
        send(s3s.at[s], s3r.at[s], b3s.at[s], b3r.at[s], far)

    def final(s):
        arrived(q3s.at[s], q3r.at[s], a3s.at[s], a3r.at[s])
        arrived(s3s.at[s], s3r.at[s], b3s.at[s], b3r.at[s])
        return ubuf[s, h] + decoded(q3r[s], s3r[s])

    def begin(s):
        @pl.loop(0, KPG // 2)
        def _(pair):
            widen(packed[s, pair], c, pair)
        multiply(s, c, False)

    def finish(s):
        arrived(packed.at[s], other.at[s], xs.at[s], xr.at[s])

        @pl.loop(0, KPG // 2)
        def _(pair):
            widen(other[s, pair], 1 - c, pair)
        multiply(s, 1 - c, True)

    left_index.wait()
    right_index.wait()
    mine.wait()
    arrived(left_hbm, left.at[1], xs.at[PASSES], xr.at[PASSES])
    for s in range(PASSES):
        begin(s)
    ready = []
    for step in range(PASSES + 4):
        if step < PASSES:
            finish(step)
            stage1_open(step)
        if 0 <= step - 1 < PASSES:
            stage1_relay(step - 1)
        if 0 <= step - 2 < PASSES:
            stage2(step - 2)
        if 0 <= step - 3 < PASSES:
            stage3(step - 3)
        if 0 <= step - 4 < PASSES:
            ready.append(final(step - 4))
    for j in range(JB):
        out[:, j * BLK:(j + 1) * BLK] = jnp.concatenate(
            [one[:, j * WIDTH:(j + 1) * WIDTH] for one in ready], axis=1)
    for copy in started:
        copy.wait_send()


def local(left_blocks, left_cols, right_blocks, right_cols):
    dma = pltpu.SemaphoreType.DMA
    vmem = pltpu.VMEM
    q1 = vmem((PASSES, 2, 6, 2, HALF, NCOL), jnp.int16)
    s1 = vmem((PASSES, 2, 6, 1, NCOL), jnp.float32)
    q2 = vmem((PASSES, 2, 3, HALF, NCOL), jnp.int16)
    s2 = vmem((PASSES, 2, 3, 1, NCOL), jnp.float32)
    q3 = vmem((PASSES, HALF, NCOL), jnp.int16)
    s3 = vmem((PASSES, 1, NCOL), jnp.float32)
    n1, n2, n3 = PASSES * 12, PASSES * 6, PASSES
    return pl.pallas_call(
        kernel,
        out_shape=jax.ShapeDtypeStruct((HALF, JB * BLK), jnp.float32),
        in_specs=[pl.BlockSpec(memory_space=pl.ANY)] * 4,
        out_specs=pl.BlockSpec(memory_space=pltpu.VMEM),
        scratch_shapes=[
            pltpu.SMEM((ROWS, 2, 2, 32), jnp.int32),
            pltpu.SMEM((2, 2, 2 * 32 * KPG), jnp.int32),
            vmem((KPG, 2, BLK, BLK), jnp.bfloat16),
            vmem((2, ROWS, 2, BLK, BLK), jnp.bfloat16),
            vmem((PASSES, KPG // 2, BLK, BLK), jnp.bfloat16),
            vmem((PASSES, KPG // 2, BLK, BLK), jnp.bfloat16),
            vmem((2 * KPG, BLK, NCOL), jnp.bfloat16),
            vmem((PASSES, 4, 4, BLK, NCOL), jnp.float32),
            vmem((PASSES, 2, HALF, NCOL), jnp.float32),
            q1, q1, s1, s1, q2, q2, s2, s2, q3, q3, s3, s3,
            dma((2,)), dma((2,)), dma((PASSES + 1,)), dma((PASSES + 1,)),
            dma((n1,)), dma((n1,)), dma((n1,)), dma((n1,)),
            dma((n2,)), dma((n2,)), dma((n2,)), dma((n2,)),
            dma((n3,)), dma((n3,)), dma((n3,)), dma((n3,)),
        ],
        compiler_params=pltpu.CompilerParams(
            collective_id=0, has_side_effects=True, vmem_limit_bytes=67_043_328),
    )(left_cols.transpose(0, 1, 3, 2), right_cols.transpose(1, 2, 0), left_blocks.reshape(ROWS, 2, BLK, BLK), right_blocks.reshape(KPG, 2, BLK, BLK))


def solution(mesh):
    return jax.shard_map(
        local,
        mesh=mesh,
        in_specs=(
            P("col", "row", "depth", None, None, None),
            P(),
            P(("col", "depth"), "row", None, None, None),
            P(),
        ),
        out_specs=P(("col", "depth"), "row"),
        check_vma=False,
    )
```

```python
import jax
import jax.numpy as jnp
from jax import lax
from jax.experimental import pallas as pl
from jax.experimental.pallas import tpu as pltpu
from jax.sharding import PartitionSpec as P

BLK = 128
JB = 4
PASSES = 2
WIDTH = BLK // PASSES
NCOL = JB * WIDTH
ROWS = 16
KPG = 8
HALF = BLK // 2
TOP = 32767.0
MESH = pl.DeviceIdType.MESH


def coded(x, axes):
    peak = jnp.maximum(jnp.max(jnp.abs(x), axis=axes, keepdims=True), 1e-33)
    whole = jnp.round(x * (TOP / peak)).astype(jnp.int32).astype(jnp.int16)
    return whole, peak.reshape(1, NCOL) * (1.0 / TOP)


def decoded(whole, scale):
    return whole.astype(jnp.int32).astype(jnp.float32) * scale


def kernel(lcols_hbm, rcols_hbm, left_hbm, right_hbm, out, lcols, rcols, right, left, packed, other, spread, acc, ubuf,
           q1s, q1r, s1s, s1r, q2s, q2r, s2s, s2r, q3s, q3r, s3s, s3r,
           lsem, isem, xs, xr, a1s, a1r, b1s, b1r, a2s, a2r, b2s, b2r, a3s, a3r, b3s, b3r):
    r = lax.axis_index("row")
    c = lax.axis_index("col")
    d = lax.axis_index("depth")
    z, y, h = d // 8, (d // 2) % 4, d % 2

    def at(zz, yy, hh):
        return (r, c, (zz % 4) * 8 + (yy % 4) * 2 + hh)

    mate, peer, far = (1 - r, c, d), (r, 1 - c, d), at(z, y, 1 - h)
    along = (
        lambda by: at(z + by, y, h),
        lambda by: at(z, y + by, h),
    )
    mine = pltpu.make_async_copy(left_hbm, left.at[0], lsem.at[0])
    margin = pltpu.make_async_copy(right_hbm, right, lsem.at[1])
    left_index = pltpu.make_async_copy(lcols_hbm.at[pl.ds(c * ROWS, ROWS)], lcols, isem.at[0])
    right_index = pltpu.make_async_copy(rcols_hbm, rcols, isem.at[1])
    margin.start()
    mine.start()
    left_index.start()
    right_index.start()

    barrier = pltpu.get_barrier_semaphore()
    peers = [mate, peer, far] + [go(by) for go in along for by in (1, 2, 3)]
    for device in peers:
        pl.semaphore_signal(barrier, inc=1, device_id=device, device_id_type=MESH)

    started = []

    def send(src, dst, ssem, rsem, device):
        copy = pltpu.make_async_remote_copy(
            src_ref=src, dst_ref=dst, send_sem=ssem, recv_sem=rsem,
            device_id=device, device_id_type=MESH)
        copy.start()
        started.append(copy)

    def arrived(src, dst, ssem, rsem):
        pltpu.make_async_remote_copy(
            src_ref=src, dst_ref=dst, send_sem=ssem, recv_sem=rsem,
            device_id=mate, device_id_type=MESH).wait_recv()

    margin.wait()
    for k in range(KPG):
        one, two = right[k, 0], right[k, 1]
        packed[0, k] = jnp.concatenate([one[:, :HALF], two[:, :HALF]], axis=1)
        packed[1, k] = jnp.concatenate([one[:, HALF:], two[:, HALF:]], axis=1)

    pl.semaphore_wait(barrier, len(peers))
    for s in range(PASSES):
        send(packed.at[s], other.at[s], xs.at[s], xr.at[s], peer)
    send(left_hbm, left.at[1], xs.at[2], xr.at[2], mate)

    lane = lax.broadcasted_iota(jnp.int32, (1, BLK), 1)
    upper = (lane >= HALF).astype(jnp.int32)

    def widen(block, group, k):
        row = group * (32 * KPG) + d * KPG + k
        j0, j1 = rcols[r, 0, row], rcols[r, 1, row]
        turned = pltpu.roll(block, HALF, 1)
        straight = jnp.where(upper == 0, j0, j1)
        crossed = jnp.where(upper == 0, j1, j0)
        for t in range(2):
            target = upper + 2 * t
            keep = (straight == target).astype(jnp.float32).astype(jnp.bfloat16)
            swap = (crossed == target).astype(jnp.float32).astype(jnp.bfloat16)
            spread[group * KPG + k, :, t * BLK:(t + 1) * BLK] = block * keep + turned * swap

    def multiply(s, group, add):
        slot = (group + r) % 2

        @pl.loop(0, ROWS // 4)
        def _(block_z):
            for block_y in range(4):
                i = block_z * 4 + block_y
                a0, a1 = lcols[i, group, 0, d], lcols[i, group, 1, d]
                lhs = jnp.concatenate([left[slot, i, 0], left[slot, i, 1]], axis=1)
                rhs = jnp.concatenate([spread[group * KPG + a0], spread[group * KPG + a1]], axis=0)
                term = jnp.dot(lhs, rhs, preferred_element_type=jnp.float32)
                if add:
                    term = term + acc[s, block_z, block_y]
                acc[s, block_z, block_y] = term

    where = (z, y)

    def own(s, part, pair, dest):
        if part == 0:
            return acc[s, dest, 2 * pair:2 * pair + 2, :HALF, :]
        return acc[s, 2 * pair:2 * pair + 2, dest, HALF:, :]

    def one(s, part, w, dest):
        if part == 0:
            return acc[s, dest, w, :HALF, :]
        return acc[s, w, dest, HALF:, :]

    def post1(s, part, slot, value, by):
        whole, scale = coded(value, (0, 1))
        q1s[s, part, slot] = whole
        s1s[s, part, slot] = scale
        n = (s * 2 + part) * 6 + slot
        send(q1s.at[s, part, slot], q1r.at[s, part, slot], a1s.at[n], a1r.at[n], along[part](by))
        send(s1s.at[s, part, slot], s1r.at[s, part, slot], b1s.at[n], b1r.at[n], along[part](by))

    def got1(s, part, slot):
        n = (s * 2 + part) * 6 + slot
        arrived(q1s.at[s, part, slot], q1r.at[s, part, slot], a1s.at[n], a1r.at[n])
        arrived(s1s.at[s, part, slot], s1r.at[s, part, slot], b1s.at[n], b1r.at[n])

    def stage1(s):
        for by in (2, 1, 3):
            for part in range(2):
                for pair in range(2):
                    post1(s, part, 2 * (by - 1) + pair, own(s, part, pair, (where[part] + by) % 4), by)

    def reduced(s, part, w):
        value = one(s, part, w, where[part])
        for first in (0, 2, 4):
            pair = first + w // 2
            value = value + decoded(q1r[s, part, pair, w % 2], s1r[s, part, pair])
        return value

    def stage2(s):
        for part in range(2):
            for slot in (4, 5, 0, 1, 2, 3):
                got1(s, part, slot)
            v = where[1 - part]
            for by in (2, 1, 3):
                whole, scale = coded(reduced(s, part, (v + by) % 4), 0)
                q2s[s, part, by - 1] = whole
                s2s[s, part, by - 1] = scale
                n = (s * 2 + part) * 3 + by - 1
                send(q2s.at[s, part, by - 1], q2r.at[s, part, by - 1], a2s.at[n], a2r.at[n], along[1 - part](by))
                send(s2s.at[s, part, by - 1], s2r.at[s, part, by - 1], b2s.at[n], b2r.at[n], along[1 - part](by))
            ubuf[s, part] = reduced(s, part, v)

    def stage3(s):
        for part in range(2):
            value = ubuf[s, part]
            for by in range(3):
                n = (s * 2 + part) * 3 + by
                arrived(q2s.at[s, part, by], q2r.at[s, part, by], a2s.at[n], a2r.at[n])
                arrived(s2s.at[s, part, by], s2r.at[s, part, by], b2s.at[n], b2r.at[n])
                value = value + decoded(q2r[s, part, by], s2r[s, part, by])
            ubuf[s, part] = value
        whole, scale = coded(ubuf[s, 1 - h], 0)
        q3s[s] = whole
        s3s[s] = scale
        send(q3s.at[s], q3r.at[s], a3s.at[s], a3r.at[s], far)
        send(s3s.at[s], s3r.at[s], b3s.at[s], b3r.at[s], far)

    def final(s):
        arrived(q3s.at[s], q3r.at[s], a3s.at[s], a3r.at[s])
        arrived(s3s.at[s], s3r.at[s], b3s.at[s], b3r.at[s])
        return ubuf[s, h] + decoded(q3r[s], s3r[s])

    def begin(s):
        @pl.loop(0, KPG)
        def _(k):
            widen(packed[s, k], c, k)
        multiply(s, c, False)

    def finish(s):
        arrived(packed.at[s], other.at[s], xs.at[s], xr.at[s])

        @pl.loop(0, KPG)
        def _(k):
            widen(other[s, k], 1 - c, k)
        multiply(s, 1 - c, True)

    left_index.wait()
    right_index.wait()
    mine.wait()
    arrived(left_hbm, left.at[1], xs.at[2], xr.at[2])
    begin(0)
    begin(1)
    finish(0)
    stage1(0)
    finish(1)
    stage1(1)
    stage2(0)
    stage3(0)
    stage2(1)
    first = final(0)
    stage3(1)
    second = final(1)
    for j in range(JB):
        out[:, j * BLK:(j + 1) * BLK] = jnp.concatenate(
            [first[:, j * WIDTH:(j + 1) * WIDTH], second[:, j * WIDTH:(j + 1) * WIDTH]], axis=1)
    for copy in started:
        copy.wait_send()


def local(left_blocks, left_cols, right_blocks, right_cols):
    dma = pltpu.SemaphoreType.DMA
    vmem = pltpu.VMEM
    q1 = vmem((PASSES, 2, 6, 2, HALF, NCOL), jnp.int16)
    s1 = vmem((PASSES, 2, 6, 1, NCOL), jnp.float32)
    q2 = vmem((PASSES, 2, 3, HALF, NCOL), jnp.int16)
    s2 = vmem((PASSES, 2, 3, 1, NCOL), jnp.float32)
    q3 = vmem((PASSES, HALF, NCOL), jnp.int16)
    s3 = vmem((PASSES, 1, NCOL), jnp.float32)
    n1, n2, n3 = PASSES * 12, PASSES * 6, PASSES
    return pl.pallas_call(
        kernel,
        out_shape=jax.ShapeDtypeStruct((HALF, JB * BLK), jnp.float32),
        in_specs=[pl.BlockSpec(memory_space=pl.ANY)] * 4,
        out_specs=pl.BlockSpec(memory_space=pltpu.VMEM),
        scratch_shapes=[
            pltpu.SMEM((ROWS, 2, 2, 32), jnp.int32),
            pltpu.SMEM((2, 2, 2 * 32 * KPG), jnp.int32),
            vmem((KPG, 2, BLK, BLK), jnp.bfloat16),
            vmem((2, ROWS, 2, BLK, BLK), jnp.bfloat16),
            vmem((PASSES, KPG, BLK, BLK), jnp.bfloat16),
            vmem((PASSES, KPG, BLK, BLK), jnp.bfloat16),
            vmem((2 * KPG, BLK, NCOL), jnp.bfloat16),
            vmem((PASSES, 4, 4, BLK, NCOL), jnp.float32),
            vmem((PASSES, 2, HALF, NCOL), jnp.float32),
            q1, q1, s1, s1, q2, q2, s2, s2, q3, q3, s3, s3,
            dma((2,)), dma((2,)), dma((3,)), dma((3,)),
            dma((n1,)), dma((n1,)), dma((n1,)), dma((n1,)),
            dma((n2,)), dma((n2,)), dma((n2,)), dma((n2,)),
            dma((n3,)), dma((n3,)), dma((n3,)), dma((n3,)),
        ],
        compiler_params=pltpu.CompilerParams(
            collective_id=0, has_side_effects=True, vmem_limit_bytes=67_043_328),
    )(left_cols.transpose(0, 1, 3, 2), right_cols.transpose(1, 2, 0), left_blocks.reshape(ROWS, 2, BLK, BLK), right_blocks.reshape(KPG, 2, BLK, BLK))


def solution(mesh):
    return jax.shard_map(
        local,
        mesh=mesh,
        in_specs=(
            P("col", "row", "depth", None, None, None),
            P(),
            P(("col", "depth"), "row", None, None, None),
            P(),
        ),
        out_specs=P(("col", "depth"), "row"),
        check_vma=False,
    )
```

```python
import jax
import jax.numpy as jnp
from jax import lax
from jax.experimental import pallas as pl
from jax.experimental.pallas import tpu as pltpu
from jax.sharding import PartitionSpec as P

BLK = 128
JB = 4
PASSES = 2
WIDTH = BLK // PASSES
NCOL = JB * WIDTH
ROWS = 16
KPG = 8
HALF = BLK // 2
TOP = 32767.0
MESH = pl.DeviceIdType.MESH


def coded(x, axes):
    peak = jnp.maximum(jnp.max(jnp.abs(x), axis=axes, keepdims=True), 1e-33)
    whole = jnp.round(x * (TOP / peak)).astype(jnp.int32).astype(jnp.int16)
    return whole, peak.reshape(1, NCOL) * (1.0 / TOP)


def decoded(whole, scale):
    return whole.astype(jnp.int32).astype(jnp.float32) * scale


def kernel(lcols_hbm, rcols_hbm, left_hbm, right_hbm, out, lcols, rcols, right, left, packed, other, spread, acc, ubuf,
           q1s, q1r, s1s, s1r, q2s, q2r, s2s, s2r,
           lsem, isem, xs, xr, a1s, a1r, b1s, b1r, a2s, a2r, b2s, b2r):
    r = lax.axis_index("row")
    c = lax.axis_index("col")
    d = lax.axis_index("depth")
    z, y, h = d // 8, (d // 2) % 4, d % 2

    def at(zz, yy, hh):
        return (r, c, (zz % 4) * 8 + (yy % 4) * 2 + hh)

    mate, peer, far = (1 - r, c, d), (r, 1 - c, d), at(z, y, 1 - h)
    along = (
        lambda by: at(z + by, y, h),
        lambda by: at(z, y + by, h),
    )
    mine = pltpu.make_async_copy(left_hbm, left.at[0], lsem.at[0])
    margin = pltpu.make_async_copy(right_hbm, right, lsem.at[1])
    left_index = pltpu.make_async_copy(lcols_hbm.at[pl.ds(c * ROWS, ROWS)], lcols, isem.at[0])
    right_index = pltpu.make_async_copy(rcols_hbm, rcols, isem.at[1])
    margin.start()
    mine.start()
    left_index.start()
    right_index.start()

    barrier = pltpu.get_barrier_semaphore()
    peers = [mate, peer, far] + [go(by) for go in along for by in (1, 2, 3)]
    peers += [at(z + by, y, 1 - h) for by in (1, 2, 3)] + [at(z, y + by, 1 - h) for by in (1, 2, 3)]
    for device in peers:
        pl.semaphore_signal(barrier, inc=1, device_id=device, device_id_type=MESH)

    started = []

    def send(src, dst, ssem, rsem, device):
        copy = pltpu.make_async_remote_copy(
            src_ref=src, dst_ref=dst, send_sem=ssem, recv_sem=rsem,
            device_id=device, device_id_type=MESH)
        copy.start()
        started.append(copy)

    def arrived(src, dst, ssem, rsem):
        pltpu.make_async_remote_copy(
            src_ref=src, dst_ref=dst, send_sem=ssem, recv_sem=rsem,
            device_id=mate, device_id_type=MESH).wait_recv()

    margin.wait()
    for k in range(KPG):
        one, two = right[k, 0], right[k, 1]
        packed[0, k] = jnp.concatenate([one[:, :HALF], two[:, :HALF]], axis=1)
        packed[1, k] = jnp.concatenate([one[:, HALF:], two[:, HALF:]], axis=1)

    pl.semaphore_wait(barrier, len(peers))
    for s in range(PASSES):
        send(packed.at[s], other.at[s], xs.at[s], xr.at[s], peer)
    send(left_hbm, left.at[1], xs.at[2], xr.at[2], mate)

    lane = lax.broadcasted_iota(jnp.int32, (1, BLK), 1)
    upper = (lane >= HALF).astype(jnp.int32)

    def widen(block, group, k):
        row = group * (32 * KPG) + d * KPG + k
        j0, j1 = rcols[r, 0, row], rcols[r, 1, row]
        turned = pltpu.roll(block, HALF, 1)
        straight = jnp.where(upper == 0, j0, j1)
        crossed = jnp.where(upper == 0, j1, j0)
        for t in range(2):
            target = upper + 2 * t
            keep = (straight == target).astype(jnp.float32).astype(jnp.bfloat16)
            swap = (crossed == target).astype(jnp.float32).astype(jnp.bfloat16)
            spread[group * KPG + k, :, t * BLK:(t + 1) * BLK] = block * keep + turned * swap

    def multiply(s, group, add):
        slot = (group + r) % 2

        @pl.loop(0, ROWS // 4)
        def _(block_z):
            for block_y in range(4):
                i = block_z * 4 + block_y
                a0, a1 = lcols[i, group, 0, d], lcols[i, group, 1, d]
                lhs = jnp.concatenate([left[slot, i, 0], left[slot, i, 1]], axis=1)
                rhs = jnp.concatenate([spread[group * KPG + a0], spread[group * KPG + a1]], axis=0)
                term = jnp.dot(lhs, rhs, preferred_element_type=jnp.float32)
                if add:
                    term = term + acc[s, block_z, block_y]
                acc[s, block_z, block_y] = term

    where = (z, y)

    def own(s, part, pair, dest):
        if part == 0:
            return acc[s, dest, 2 * pair:2 * pair + 2, :HALF, :]
        return acc[s, 2 * pair:2 * pair + 2, dest, HALF:, :]

    def one(s, part, w, dest):
        if part == 0:
            return acc[s, dest, w, :HALF, :]
        return acc[s, w, dest, HALF:, :]

    def post1(s, part, slot, value, by):
        whole, scale = coded(value, (0, 1))
        q1s[s, part, slot] = whole
        s1s[s, part, slot] = scale
        n = (s * 2 + part) * 6 + slot
        send(q1s.at[s, part, slot], q1r.at[s, part, slot], a1s.at[n], a1r.at[n], along[part](by))
        send(s1s.at[s, part, slot], s1r.at[s, part, slot], b1s.at[n], b1r.at[n], along[part](by))

    def got1(s, part, slot):
        n = (s * 2 + part) * 6 + slot
        arrived(q1s.at[s, part, slot], q1r.at[s, part, slot], a1s.at[n], a1r.at[n])
        arrived(s1s.at[s, part, slot], s1r.at[s, part, slot], b1s.at[n], b1r.at[n])

    def stage1(s):
        for by in (2, 1, 3):
            for part in range(2):
                for pair in range(2):
                    post1(s, part, 2 * (by - 1) + pair, own(s, part, pair, (where[part] + by) % 4), by)

    def reduced(s, part, w):
        value = one(s, part, w, where[part])
        for first in (0, 2, 4):
            pair = first + w // 2
            value = value + decoded(q1r[s, part, pair, w % 2], s1r[s, part, pair])
        return value

    def stage2(s):
        for part in range(2):
            for slot in (4, 5, 0, 1, 2, 3):
                got1(s, part, slot)
            v = where[1 - part]
            for by in (2, 1, 3, 0):
                value = reduced(s, part, (v + by) % 4)
                whole, scale = coded(value, 0)
                q2s[s, part, by] = whole
                s2s[s, part, by] = scale
                if by == 0:
                    ubuf[s, part] = value
        for part, first in ((1 - h, 4), (h, 0)):
            for by in (2, 1, 3, 0):
                if first + by:
                    n = s * 8 + first + by
                    device = at(z + by * part, y + by * (1 - part), part)
                    send(q2s.at[s, part, by], q2r.at[s, first + by], a2s.at[n], a2r.at[n], device)
                    send(s2s.at[s, part, by], s2r.at[s, first + by], b2s.at[n], b2r.at[n], device)

    def final(s):
        value = ubuf[s, h]
        for slot in (1, 3, 2, 4, 5, 7, 6):
            n = s * 8 + slot
            arrived(q2r.at[s, slot], q2r.at[s, slot], a2s.at[n], a2r.at[n])
            arrived(s2r.at[s, slot], s2r.at[s, slot], b2s.at[n], b2r.at[n])
            value = value + decoded(q2r[s, slot], s2r[s, slot])
        return value

    def begin(s):
        @pl.loop(0, KPG)
        def _(k):
            widen(packed[s, k], c, k)
        multiply(s, c, False)

    def finish(s):
        arrived(packed.at[s], other.at[s], xs.at[s], xr.at[s])

        @pl.loop(0, KPG)
        def _(k):
            widen(other[s, k], 1 - c, k)
        multiply(s, 1 - c, True)

    left_index.wait()
    right_index.wait()
    mine.wait()
    arrived(left_hbm, left.at[1], xs.at[2], xr.at[2])
    begin(0)
    begin(1)
    finish(0)
    stage1(0)
    finish(1)
    stage1(1)
    stage2(0)
    stage2(1)
    first = final(0)
    second = final(1)
    for j in range(JB):
        out[:, j * BLK:(j + 1) * BLK] = jnp.concatenate(
            [first[:, j * WIDTH:(j + 1) * WIDTH], second[:, j * WIDTH:(j + 1) * WIDTH]], axis=1)
    for copy in started:
        copy.wait_send()


def local(left_blocks, left_cols, right_blocks, right_cols):
    dma = pltpu.SemaphoreType.DMA
    vmem = pltpu.VMEM
    q1 = vmem((PASSES, 2, 6, 2, HALF, NCOL), jnp.int16)
    s1 = vmem((PASSES, 2, 6, 1, NCOL), jnp.float32)
    q2s = vmem((PASSES, 2, 4, HALF, NCOL), jnp.int16)
    s2s = vmem((PASSES, 2, 4, 1, NCOL), jnp.float32)
    q2r = vmem((PASSES, 8, HALF, NCOL), jnp.int16)
    s2r = vmem((PASSES, 8, 1, NCOL), jnp.float32)
    n1, n2 = PASSES * 12, PASSES * 8
    return pl.pallas_call(
        kernel,
        out_shape=jax.ShapeDtypeStruct((HALF, JB * BLK), jnp.float32),
        in_specs=[pl.BlockSpec(memory_space=pl.ANY)] * 4,
        out_specs=pl.BlockSpec(memory_space=pltpu.VMEM),
        scratch_shapes=[
            pltpu.SMEM((ROWS, 2, 2, 32), jnp.int32),
            pltpu.SMEM((2, 2, 2 * 32 * KPG), jnp.int32),
            vmem((KPG, 2, BLK, BLK), jnp.bfloat16),
            vmem((2, ROWS, 2, BLK, BLK), jnp.bfloat16),
            vmem((PASSES, KPG, BLK, BLK), jnp.bfloat16),
            vmem((PASSES, KPG, BLK, BLK), jnp.bfloat16),
            vmem((2 * KPG, BLK, NCOL), jnp.bfloat16),
            vmem((PASSES, 4, 4, BLK, NCOL), jnp.float32),
            vmem((PASSES, 2, HALF, NCOL), jnp.float32),
            q1, q1, s1, s1, q2s, q2r, s2s, s2r,
            dma((2,)), dma((2,)), dma((3,)), dma((3,)),
            dma((n1,)), dma((n1,)), dma((n1,)), dma((n1,)),
            dma((n2,)), dma((n2,)), dma((n2,)), dma((n2,)),
        ],
        compiler_params=pltpu.CompilerParams(
            collective_id=0, has_side_effects=True, vmem_limit_bytes=67_043_328),
    )(left_cols.transpose(0, 1, 3, 2), right_cols.transpose(1, 2, 0), left_blocks.reshape(ROWS, 2, BLK, BLK), right_blocks.reshape(KPG, 2, BLK, BLK))


def solution(mesh):
    return jax.shard_map(
        local,
        mesh=mesh,
        in_specs=(
            P("col", "row", "depth", None, None, None),
            P(),
            P(("col", "depth"), "row", None, None, None),
            P(),
        ),
        out_specs=P(("col", "depth"), "row"),
        check_vma=False,
    )
```
